256 devices in a mesh: row: 4 (over y_hi, core), col: 8 (over z), seq: 8 (over x, y_lo).
Axes of the slice: x: 4, y: 4 (y_hi: 2, y_lo: 2; y = y_hi * 2 + y_lo), z: 8, core: 2. Of those that a mesh axis runs over, the one named last changes fastest.
Arguments:
- queries: bfloat16 [4, 2048, 8192], P('row', 'seq', 'col'), may hold values from -120 to 120
- rotated_key_heads: bfloat16 [4, 2048, 1024], P('row', 'seq', 'col'), may hold values from -7 to 7
- value_head_states: bfloat16 [4, 2048, 1024], P('row', 'seq', 'col'), may hold values from -6 to 6
- document_index: int32 [4, 2048], P('row'), may hold values from 0 to 3, never falling along the last dimension, each value on 1 to 1024 neighbouring positions
- output_projection_weight: bfloat16 [8192, 8192], P('col', 'row'), may hold values from -0.1875 to 0.1875
- frozen_down_factor: bfloat16 [8192, 256], P('col'), may hold values from -0.1875 to 0.1875
- trained_up_factor: bfloat16 [256, 8192], P(None, 'row'), may hold values from -0.125 to 0.125
- correction_tiles: bfloat16 [4, 8, 2, 128, 128], P('row', 'col'), may hold values from -1.1953125 to 1.1953125
- tile_placement: int32 [4, 8, 2, 2], P('row', 'col'), may hold values from 0 to 15, as said below
- cotangent: bfloat16 [4, 2048, 8192], P(None, 'seq', ('row', 'col')), may hold values from -0.06591797 to 0.06591797
Outputs:
- projected: bfloat16 [4, 2048, 8192], P(None, 'seq', ('row', 'col'))
- up_factor_gradient: float32 [256, 8192], P(None, 'row')
- grad_tiles: float32 [4, 8, 2, 128, 128], P('row', 'col')
The draws below stay inside these ranges and needn't reach their ends.
Inputs may be any that keep to these rules, and one draw needn't show every extreme that they name: `tile_placement`: inside one block of the weight grid the 2 tiles are different; entry 0 is a tile row below 8, entry 1 a tile column below 16.
All inputs are finite; a program needn't handle non-finite values.
Results may differ from the reference program's by a relative error of at most 0.0054.
Values may be sent and summed in bfloat16 or wider, within the bound.
A program may use at most 128 MiB of HBM per device.

```python
import math
import jax
import jax.numpy as jnp
import numpy as np
from jax import lax

MODEL_WIDTH = 8192
QUERY_HEADS = 64
KEY_VALUE_HEADS = 8
HEAD_WIDTH = 128
CORRECTION_RANK = 256
TILE = 128
SEQUENCE_LENGTH = 2048
SEQUENCE_COUNT = 4
DTB = 2
N_ROW = 4
N_COL = 8


def query_key_pair(key):
    random_key_query = jax.random.fold_in(key, 101)
    random_key_for_keys = jax.random.fold_in(key, 102)
    query_group_width = QUERY_HEADS // KEY_VALUE_HEADS
    random_key_draw = jnp.clip(jax.random.normal(random_key_for_keys, (SEQUENCE_COUNT, SEQUENCE_LENGTH, KEY_VALUE_HEADS, HEAD_WIDTH), jnp.float32), -5.0, 5.0)
    random_query_draw = jnp.clip(2.0 * jax.random.normal(random_key_query, (SEQUENCE_COUNT, SEQUENCE_LENGTH, KEY_VALUE_HEADS, query_group_width, HEAD_WIDTH), jnp.float32), -12.0, 12.0)
    return (random_query_draw.reshape(SEQUENCE_COUNT, SEQUENCE_LENGTH, QUERY_HEADS * HEAD_WIDTH), random_key_draw.reshape(SEQUENCE_COUNT, SEQUENCE_LENGTH, KEY_VALUE_HEADS * HEAD_WIDTH))


def draw_queries(key, part):
    return query_key_pair(key)[0].astype(jnp.bfloat16)


def draw_rotated_key_heads(key, part):
    return query_key_pair(key)[1].astype(jnp.bfloat16)


def to_front(order, wanted):
    position = jnp.argmax((order == wanted).astype(jnp.int32))
    first = order[0]
    return order.at[position].set(first).at[0].set(wanted)


def draw_tile_placement(key, part):
    in_tiles = QUERY_HEADS * HEAD_WIDTH // N_COL // TILE
    out_tiles = MODEL_WIDTH // N_ROW // TILE
    total = in_tiles * out_tiles
    block_keys = jax.random.split(jax.random.fold_in(key, 303), N_ROW * N_COL)
    orders = jax.vmap(lambda single: jax.random.permutation(single, total))(block_keys).astype(jnp.int32)
    orders = orders.at[0].set(to_front(orders[0], total - 1))
    last_block = N_ROW * N_COL - 1
    orders = orders.at[last_block].set(to_front(orders[last_block], 0))
    chosen = orders[:, :DTB].reshape(N_ROW, N_COL, DTB)
    return jnp.stack([chosen // out_tiles, chosen % out_tiles], axis=-1).astype(jnp.int32)


def level_of(key, extent, cuts, least, high):
    def one(dim, blocks):
        heights = jax.random.uniform(jax.random.fold_in(jax.random.fold_in(key, 6), dim), (blocks,), jnp.float32, least / len(cuts), high / len(cuts))
        return jnp.repeat(jnp.exp(heights), extent[dim] // blocks).reshape((-1,) + (1,) * (len(extent) - dim - 1))

    gain = one(*cuts[0])
    for cut in cuts[1:]:
        gain = gain * one(*cut)
    return gain


def split_up(amount, total, most, lean):
    weights = [(1 << 20) // math.isqrt(standing ** lean) + 1 for standing in range(2, amount + 1)]
    rest, holding = total - most - (amount - 1), [1] * (amount - 1)
    while rest > 0:
        free = [i for i in range(amount - 1) if holding[i] < most]
        mass, remaining = sum([weights[i] for i in free]), rest
        for i in free:
            addition = min(most - holding[i], max(1, remaining * weights[i] // mass), rest)
            holding[i] = holding[i] + addition
            rest = rest - addition
    return np.array([most] + holding)


def uneven_parts(own_key, number_of, total, most, lean):
    if number_of == 2:
        one = jax.random.randint(own_key, (), max(1, total - most), min(most, total - 1) + 1)
        return jnp.stack([one, total - one])
    sizes = jnp.asarray(split_up(number_of, total, most, lean), jnp.int32)
    pairs = (number_of - 1) // 2
    donor, sink = sizes[1:1 + 2 * pairs:2], sizes[2:2 + 2 * pairs:2]
    margin = jnp.minimum(donor - 1, most - sink)
    moved = jax.random.randint(jax.random.fold_in(own_key, 1), (pairs,), 0, 1 << 20) % (margin + 1)
    sizes = sizes.at[1:1 + 2 * pairs:2].set(donor - moved).at[2:2 + 2 * pairs:2].set(sink + moved)
    return sizes[jax.random.permutation(jax.random.fold_in(own_key, 2), number_of)]


def bell_draw(stream_key, dims, scale, most, cuts=(), kind=jnp.bfloat16):
    result = scale * jax.random.normal(stream_key, dims, jnp.float32)
    if cuts:
        result = result * level_of(stream_key, dims, cuts, -0.22, 0.18)
    return jnp.clip(result, -most, most).astype(kind)


def setup_inputs(seed: int = 0) -> dict:
    keys = jax.random.split(jax.random.key(seed), 11)
    queries = draw_queries(jax.random.fold_in(keys[10], 71), 0)
    rotated_key_heads = draw_rotated_key_heads(jax.random.fold_in(keys[10], 71), 0)
    value_head_states = bell_draw(keys[2], (SEQUENCE_COUNT, SEQUENCE_LENGTH, KEY_VALUE_HEADS * HEAD_WIDTH), 1.0, 6.0, ((0, 4), (1, 8), (2, 8)))
    document_index = jax.vmap(lambda own: jnp.searchsorted(jnp.cumsum(uneven_parts(own, 4, SEQUENCE_LENGTH, SEQUENCE_LENGTH // 2, 0)), jnp.arange(SEQUENCE_LENGTH), side="right"))(jax.random.split(keys[3], SEQUENCE_COUNT)).reshape((SEQUENCE_COUNT, SEQUENCE_LENGTH)).astype(jnp.int32)
    output_projection_weight = bell_draw(keys[4], (QUERY_HEADS * HEAD_WIDTH, MODEL_WIDTH), (QUERY_HEADS * HEAD_WIDTH // 8) ** -0.5, 0.1875, ((0, 8), (1, 4)))
    frozen_down_factor = bell_draw(keys[5], (QUERY_HEADS * HEAD_WIDTH, CORRECTION_RANK), (QUERY_HEADS * HEAD_WIDTH // 8) ** -0.5, 0.1875, ((0, 8),))
    trained_up_factor = bell_draw(keys[6], (CORRECTION_RANK, MODEL_WIDTH), (8 * CORRECTION_RANK) ** -0.5, 0.125, ((1, 4),))
    correction_tiles = bell_draw(keys[7], (N_ROW, N_COL, DTB, TILE, TILE), 0.2, 1.1953125, ((0, 4), (1, 8)))
    tile_placement = draw_tile_placement(jax.random.fold_in(keys[10], 71), 0)
    cotangent = bell_draw(keys[9], (SEQUENCE_COUNT, SEQUENCE_LENGTH, MODEL_WIDTH), ((SEQUENCE_COUNT * SEQUENCE_LENGTH) ** -0.5), 0.06591797, ((1, 8), (2, 32)))
    return {"queries": queries, "rotated_key_heads": rotated_key_heads, "value_head_states": value_head_states, "document_index": document_index, "output_projection_weight": output_projection_weight, "frozen_down_factor": frozen_down_factor, "trained_up_factor": trained_up_factor, "correction_tiles": correction_tiles, "tile_placement": tile_placement, "cotangent": cotangent}


low_rank_factor = 2.0


def one_head(operands):
    query_h, key_h, value_h, documents = operands
    score_scale = HEAD_WIDTH ** -0.5
    positions = jnp.arange(SEQUENCE_LENGTH, dtype=jnp.int32)
    causal = positions[None, :] <= positions[:, None]
    scores = jnp.einsum("qgd,sd->gqs", query_h.astype(jnp.float32), key_h.astype(jnp.float32), precision=lax.Precision.HIGHEST) * score_scale
    visible = (causal & (documents[None, :] == documents[:, None]))[None]
    row_max = jnp.max(jnp.where(visible, scores, -jnp.inf), axis=-1, keepdims=True)
    weights = jnp.exp(jnp.where(visible, scores - row_max, -jnp.inf))
    row_total = jnp.sum(weights, axis=-1)
    rounded = lax.optimization_barrier(weights.astype(jnp.bfloat16))
    mixed_rows = jnp.einsum("gqs,sd->qgd", rounded.astype(jnp.float32), value_h.astype(jnp.float32), precision=lax.Precision.HIGHEST)
    return (mixed_rows / row_total.T[:, :, None]).astype(jnp.bfloat16)


def reference(queries, rotated_key_heads, value_head_states, document_index, output_projection_weight, frozen_down_factor, trained_up_factor, correction_tiles, tile_placement, cotangent):
    query_group_width = QUERY_HEADS // KEY_VALUE_HEADS
    sequence_rows = queries.shape[0]
    query_head_matrix = queries.reshape(sequence_rows, SEQUENCE_LENGTH, KEY_VALUE_HEADS, query_group_width, HEAD_WIDTH).transpose(0, 2, 1, 3, 4).reshape(sequence_rows * KEY_VALUE_HEADS, SEQUENCE_LENGTH, query_group_width, HEAD_WIDTH)
    key_head_matrix = rotated_key_heads.reshape(sequence_rows, SEQUENCE_LENGTH, KEY_VALUE_HEADS, HEAD_WIDTH).transpose(0, 2, 1, 3).reshape(sequence_rows * KEY_VALUE_HEADS, SEQUENCE_LENGTH, HEAD_WIDTH)
    value_head_matrix = value_head_states.reshape(sequence_rows, SEQUENCE_LENGTH, KEY_VALUE_HEADS, HEAD_WIDTH).transpose(0, 2, 1, 3).reshape(sequence_rows * KEY_VALUE_HEADS, SEQUENCE_LENGTH, HEAD_WIDTH)
    document_tiled = jnp.repeat(document_index, KEY_VALUE_HEADS, axis=0)
    attention_output = lax.map(one_head, (query_head_matrix, key_head_matrix, value_head_matrix, document_tiled))
    attention_output = attention_output.reshape(sequence_rows, KEY_VALUE_HEADS, SEQUENCE_LENGTH, query_group_width, HEAD_WIDTH).transpose(0, 2, 1, 3, 4).reshape(sequence_rows, SEQUENCE_LENGTH, QUERY_HEADS * HEAD_WIDTH)
    token_count = sequence_rows * SEQUENCE_LENGTH
    flattened_rows = attention_output.reshape(token_count, QUERY_HEADS * HEAD_WIDTH)
    frozen_product = jnp.dot(flattened_rows, output_projection_weight, preferred_element_type=jnp.float32)
    low_rank_inner = jnp.dot(flattened_rows, frozen_down_factor, preferred_element_type=jnp.float32).astype(jnp.bfloat16)
    low_rank_product = jnp.dot(low_rank_inner, trained_up_factor, preferred_element_type=jnp.float32)
    in_block = QUERY_HEADS * HEAD_WIDTH // N_COL
    out_block = MODEL_WIDTH // N_ROW
    row_ids = jnp.arange(N_ROW, dtype=jnp.int32)[:, None, None]
    col_ids = jnp.arange(N_COL, dtype=jnp.int32)[None, :, None]
    in_start = (col_ids * in_block + tile_placement[..., 0] * TILE).reshape(-1).astype(jnp.int32)
    out_start = (row_ids * out_block + tile_placement[..., 1] * TILE).reshape(-1).astype(jnp.int32)
    offsets = jnp.arange(TILE, dtype=jnp.int32)
    in_index = in_start[:, None] + offsets[None, :]
    out_index = out_start[:, None] + offsets[None, :]
    tile_values = correction_tiles.reshape(-1, TILE, TILE).astype(jnp.float32)
    picked = flattened_rows[:, in_index].astype(jnp.float32)
    tile_terms = jnp.einsum("tni,nio->tno", picked, tile_values, precision=lax.Precision.HIGHEST)
    tile_sparse_piece = jnp.zeros((token_count, MODEL_WIDTH), jnp.float32).at[:, out_index].add(tile_terms)
    projected = (frozen_product + low_rank_factor * low_rank_product + tile_sparse_piece).astype(jnp.bfloat16).reshape(sequence_rows, SEQUENCE_LENGTH, MODEL_WIDTH)
    output_gradient_rows = cotangent.reshape(token_count, MODEL_WIDTH)
    up_factor_gradient = low_rank_factor * jnp.dot(low_rank_inner.T, output_gradient_rows, preferred_element_type=jnp.float32)
    cot_picked = output_gradient_rows.astype(jnp.float32)[:, out_index]
    grad_tiles = jnp.einsum("tni,tno->nio", picked, cot_picked, precision=lax.Precision.HIGHEST)
    grad_tiles = grad_tiles.reshape(N_ROW, N_COL, DTB, TILE, TILE)
    return projected, up_factor_gradient, grad_tiles
```

```python
import functools

import jax
import jax.numpy as jnp
from jax import lax
from jax.experimental import pallas as pl
from jax.experimental.pallas import tpu as pltpu
from jax.sharding import PartitionSpec as P

HEAD_WIDTH = 128
TILE = 128
MESH = pl.DeviceIdType.MESH
BF = jnp.bfloat16
F32 = jnp.float32
LOW_RANK_FACTOR = 2.0
EXP_SCALE = HEAD_WIDTH ** -0.5 * 1.4426950408889634
HIDDEN = -1e30


def dot(a, b, dims=((1,), (0,))):
    return lax.dot_general(a, b, (dims, ((), ())), preferred_element_type=F32)


def kernel(
    place, doc, q, k_hbm, v_hbm, w_hbm, d_hbm, u_hbm, t_hbm, cot_hbm,
    out, up_out, gt_out,
    kwin, vwin, bias, attn, cotall, w, d, u, tiles, cblk, snd, rcv, choice, picked, picked_t, lr_part, lr_recv, lr_full,
    sum_src, sum_recv, up_full, gt_full,
    kv_s, kv_r, loc, cot_s, cot_r, row_s, row_r, rs_s, rs_r, lr_s, lr_r, lb_s, lb_r, lw_s, lw_r,
    ss_s, ss_r, uz_s, uz_r, us_s, us_r, gs_s, gs_r,
):
    r, c, s = lax.axis_index("row"), lax.axis_index("col"), lax.axis_index("seq")

    def remote(src, dst, send, recv, row=None, col=None, seq=None):
        return pltpu.make_async_remote_copy(
            src_ref=src,
            dst_ref=dst,
            send_sem=send,
            recv_sem=recv,
            device_id=(r if row is None else row, c if col is None else col, s if seq is None else seq),
            device_id_type=MESH,
        )

    def mul(x, n):
        return pl.multiple_of(x * n, n)

    barrier = pltpu.get_barrier_semaphore()
    for o in range(1, 8):
        pl.semaphore_signal(barrier, inc=1, device_id=(r, c, (s + o) % 8), device_id_type=MESH)
        pl.semaphore_signal(barrier, inc=1, device_id=(r, (c + o) % 8, s), device_id_type=MESH)
    for o in range(1, 4):
        pl.semaphore_signal(barrier, inc=1, device_id=((r + o) % 4, c, s), device_id_type=MESH)
    pl.semaphore_wait(barrier, 17)

    kv = []
    for j in (1, 2, 3, 4):
        at = pl.ds((4 - j) * 256, 256)
        kv.append(remote(k_hbm, kwin.at[at], kv_s.at[j - 1, 0], kv_r.at[j - 1, 0], seq=(s + j) % 8))
        kv.append(remote(v_hbm, vwin.at[at], kv_s.at[j - 1, 1], kv_r.at[j - 1, 1], seq=(s + j) % 8))
        kv[-2].start()
        kv[-1].start()

    cot_order = [[(1, 0), (1, 1), (2, 0), (2, 1), (3, 0), (3, 1), (4, 0)],
                 [(1, 1), (1, 0), (2, 1), (2, 0), (3, 1), (3, 0), (4, 1)]]
    signs = (1, -1)

    def cot_copy(way, m):
        step, half = cot_order[way][m]
        owner = (c - signs[way] * (step - 1) + 8) % 8
        rows = pl.ds(half * 512, 512)
        src = cot_hbm.at[rows] if step == 1 else cotall.at[owner, rows]
        return remote(src, cotall.at[owner, rows], cot_s.at[way, m], cot_r.at[way, m],
                      col=(c + signs[way] + 8) % 8)

    cot = [[cot_copy(way, m) for m in range(7)] for way in range(2)]
    for m in range(2):
        for way in range(2):
            cot[way][m].start()

    def cot_forward(m):
        for way in range(2):
            cot[way][m].wait_recv()
            cot[way][m + 2].start()

    locals_ = [
        pltpu.make_async_copy(src, dst, loc.at[i])
        for i, (src, dst) in enumerate(
            (
                (k_hbm, kwin.at[pl.ds(1024, 256)]),
                (v_hbm, vwin.at[pl.ds(1024, 256)]),
                (d_hbm, d),
                (cot_hbm, cotall.at[c]),
                (t_hbm, tiles),
                (u_hbm.at[:, pl.ds(mul(c, 256), 256)], u),
                (w_hbm, w),
            )
        )
    ]
    for copy in locals_:
        copy.start()

    own_doc = doc[:, pl.ds(mul(s, 256), 256)].astype(F32)
    column = jnp.broadcast_to(own_doc, (128, 256)).T[:, :1]
    for slot in range(5):
        block = s - 4 + slot
        key_doc = doc[:, pl.ds(mul((block + 8) % 8, 256), 256)].astype(F32)
        key_at = block * 256 + lax.broadcasted_iota(jnp.int32, (256, 256), 1)
        query_at = s * 256 + lax.broadcasted_iota(jnp.int32, (256, 256), 0)
        seen = (key_at >= 0) & (key_at <= query_at) & (column == key_doc)
        bias[:, slot * 256 : slot * 256 + 256] = jnp.where(seen, 0.0, HIDDEN)

    for t in range(2):
        row = lax.broadcasted_iota(jnp.int32, (128, 1024), 0)
        lane = lax.broadcasted_iota(jnp.int32, (128, 1024), 1)
        wanted = jnp.full((128, 1024), place[t, 0], jnp.int32) * 128 + row
        choice[t * 128 : t * 128 + 128, :] = jnp.where(lane == wanted, 1.0, 0.0).astype(BF)

    locals_[0].wait()
    locals_[1].wait()
    for copy in kv[:4]:
        copy.wait_recv()
    cot_forward(0)
    for copy in kv[4:]:
        copy.wait_recv()

    own_rows = pl.ds(mul(r, 256), 256)

    def head(h, carry):
        at = pl.ds(mul(h, 128), 128)
        scores = dot(q[:, at], kwin[...], ((1,), (1,))) + bias[...]
        top = jnp.max(scores, axis=1, keepdims=True)
        probs = jnp.exp2((scores - top) * EXP_SCALE)
        total = jnp.sum(probs, axis=1, keepdims=True)
        mixed = dot(probs.astype(BF), vwin[...])
        attn[own_rows, at] = (mixed / total).astype(BF)
        return carry

    sibling, opposite = r + 1 - 2 * (r % 2), (r + 2) % 4
    shared, crossed, relayed = [], [], []
    for p in range(4):
        lanes = pl.ds(p * 256, 256)
        mine = attn.at[own_rows, lanes]
        other = attn.at[pl.ds(mul(opposite, 256), 256), lanes]
        shared.append(remote(mine, mine, row_s.at[0, p], row_r.at[0, p], row=sibling))
        crossed.append(remote(mine, mine, row_s.at[1, p], row_r.at[1, p], row=opposite))
        relayed.append(remote(other, other, row_s.at[2, p], row_r.at[2, p], row=sibling))

    def relay(p):
        crossed[p].wait_recv()
        relayed[p].start()

    for p in range(4):
        lax.fori_loop(2 * p, 2 * p + 2, head, 0)
        crossed[p].start()
        shared[p].start()
        if p == 0:
            cot_forward(1)
        if p == 2:
            cot_forward(2)

    locals_[2].wait()
    lr_part[...] = dot(attn[own_rows, :], d[...]).astype(BF).reshape(8, 32, 256)
    lr = [
        remote(lr_part.at[(c + o) % 8], lr_recv.at[o - 1], lr_s.at[o - 1], lr_r.at[o - 1], col=(c + o) % 8)
        for o in range(1, 8)
    ]
    for copy in lr:
        copy.start()
    relay(0)
    relay(1)
    for copy in lr:
        copy.wait_recv()
    piece_at = pl.ds(mul(c, 32), 32)
    lr_full[r, piece_at, :] = (lr_part[c].astype(F32) + jnp.sum(lr_recv[...].astype(F32), axis=0)).astype(BF)
    piece = lr_full.at[r, piece_at]
    lb = [remote(piece, piece, lb_s.at[o - 1], lb_r.at[o - 1], col=(c + o) % 8) for o in range(1, 8)]
    for copy in lb:
        copy.start()
    cot_forward(3)
    relay(2)
    relay(3)
    for copy in lb:
        copy.wait_recv()
    lw = [remote(lr_full.at[r], lr_full.at[r], lw_s.at[o - 1], lw_r.at[o - 1], row=(r + o) % 4) for o in range(1, 4)]
    for copy in lw:
        copy.start()
    cot_forward(4)

    for copy in shared + relayed:
        copy.wait_recv()
    for copy in locals_[3:]:
        copy.wait()

    def pick(h, carry):
        rows = pl.ds(mul(h, 512), 512)
        picked[rows, :] = dot(attn[rows, :], choice[...], ((1,), (1,))).astype(BF)
        picked_t[:, rows] = dot(choice[...], attn[rows, :], ((1,), (1,))).astype(BF)
        return carry

    lax.fori_loop(0, 2, pick, 0)

    def partial(o):
        block = (c + o) % 8
        grid = []
        for t in range(2):
            at = jnp.full((128, 128), place[t, 1], jnp.int32)
            tile = tiles[t].astype(F32)
            grid.append(
                jnp.concatenate([jnp.where(at == 2 * block + i, tile, 0.0) for i in range(2)], axis=1)
            )
        placed = jnp.concatenate(grid, axis=0).astype(BF)
        lanes = pl.ds(mul(block, 256), 256)

        def half(h, carry):
            rows = pl.ds(mul(h, 512), 512)
            cblk[o, rows, :] = dot(attn[rows, :], w[:, lanes]) + dot(picked[rows, :], placed)
            return carry

        lax.fori_loop(0, 2, half, 0)

    def rs_order(way):
        p, n = (0, 1) if way == 0 else (1, 0)
        return [(1, p), (2, n), (2, p), (3, n), (3, p), (4, n), (4, p)]

    rs = [
        [
            remote(snd.at[way, m], rcv.at[way, m], rs_s.at[way, m], rs_r.at[way, m], col=(c + signs[way] + 8) % 8)
            for m in range(7)
        ]
        for way in range(2)
    ]

    def rs_send(m):
        for way in range(2):
            step, half = rs_order(way)[m]
            o = (signs[way] * (5 - step)) % 8
            if m >= 2:
                rs[way][m - 2].wait_recv()

            def chunk(i, carry):
                rows = pl.ds(mul(i, 128), 128)
                value = cblk[o, pl.ds(half * 512 + mul(i, 128), 128), :]
                if m >= 2:
                    value = value + rcv[way, m - 2, rows, :].astype(F32)
                snd[way, m, rows, :] = value.astype(BF)
                return carry

            lax.fori_loop(0, 4, chunk, 0)
            rs[way][m].start()

    partial(4)
    rs_send(0)
    partial(3)
    partial(5)
    rs_send(1)

    for copy in lw:
        copy.wait_recv()
    up_piece = LOW_RANK_FACTOR * dot(lr_full[...].reshape(1024, 256), cotall[c], ((0,), (0,)))
    sum_src[:, :, :256] = up_piece.reshape(8, 32, 256)
    partial(2)
    partial(6)
    for m in (5, 6):
        for way in range(2):
            cot[way][m].wait_recv()
    rs_send(2)

    def tile_grads(owner, carry):
        grads = dot(picked_t[...], cotall[owner])
        kept = []
        for t in range(2):
            value = carry[t]
            for i in range(2):
                at = jnp.full((128, 128), place[t, 1], jnp.int32)
                part = grads[t * 128 : t * 128 + 128, i * 128 : i * 128 + 128]
                value = jnp.where(at == 2 * owner + i, part, value)
            kept.append(value)
        return tuple(kept)

    grads = lax.fori_loop(0, 8, tile_grads, (jnp.zeros((128, 128), F32),) * 2)
    for t in range(2):
        sum_src[t * 4 : t * 4 + 4, :, 256:] = grads[t].reshape(4, 32, 128)
    ss = [
        remote(sum_src.at[(s + o) % 8], sum_recv.at[o - 1], ss_s.at[o - 1], ss_r.at[o - 1], seq=(s + o) % 8)
        for o in range(1, 8)
    ]
    for copy in ss:
        copy.start()
    rs_send(3)
    partial(1)
    partial(7)
    for copy in ss:
        copy.wait_recv()
    total = sum_src[s] + jnp.sum(sum_recv[...], axis=0)
    seq_rows = pl.ds(mul(s, 32), 32)
    col_lanes = pl.ds(mul(c, 256), 256)
    up_full[seq_rows, col_lanes] = total[:, :256].astype(BF)
    gt_full[seq_rows, :] = total[:, 256:]
    up_at, gt_at = up_full.at[seq_rows, col_lanes], gt_full.at[seq_rows]
    uz = [remote(up_at, up_at, uz_s.at[o - 1], uz_r.at[o - 1], col=(c + o) % 8) for o in range(1, 8)]
    gs = [remote(gt_at, gt_at, gs_s.at[o - 1], gs_r.at[o - 1], seq=(s + o) % 8) for o in range(1, 8)]
    for copy in uz + gs:
        copy.start()
    rs_send(4)
    partial(0)

    def low_rank_half(h, carry):
        rows = pl.ds(mul(h, 512), 512)
        inner = lr_full[pl.ds(2 * h, 2)].reshape(512, 256)
        cblk[0, rows, :] = cblk[0, rows, :] + LOW_RANK_FACTOR * dot(inner, u[...])
        return carry

    lax.fori_loop(0, 2, low_rank_half, 0)
    for copy in uz:
        copy.wait_recv()
    seq_at = up_full.at[seq_rows]
    us = [remote(seq_at, seq_at, us_s.at[o - 1], us_r.at[o - 1], seq=(s + o) % 8) for o in range(1, 8)]
    for copy in us:
        copy.start()
    rs_send(5)
    rs_send(6)
    for copy in us + gs:
        copy.wait_recv()
    gt_out[...] = gt_full[...]
    up_copy = pltpu.make_async_copy(up_full, up_out, loc.at[0])
    up_copy.start()
    for m in (5, 6):
        for way in range(2):
            rs[way][m].wait_recv()

    def finish(i, carry):
        for half in range(2):
            rows = pl.ds(mul(i, 128), 128)
            at = pl.ds(half * 512 + mul(i, 128), 128)
            there = [rcv[way, 6 if half == way else 5, rows, :].astype(F32) for way in range(2)]
            out[at, :] = (cblk[0, at, :] + (there[0] + there[1])).astype(BF)
        return carry

    lax.fori_loop(0, 4, finish, 0)
    up_copy.wait()
    for copy in kv + cot[0] + cot[1] + shared + crossed + relayed + lr + lb + lw + rs[0] + rs[1] + ss + uz + gs + us:
        copy.wait_send()


def hand_over(out, up_grad, tile_grad, out_to, up_to, tile_to):
    out_to[...] = out[...]
    up_to[...] = up_grad[...].astype(F32)
    tile_to[...] = tile_grad[...]


def local(queries, keys, values, documents, weight, down, up, tiles, placement, cotangent):
    dma = pltpu.SemaphoreType.DMA
    vmem = pltpu.VMEM
    anywhere = pl.BlockSpec(memory_space=pl.ANY)
    in_vmem = pl.BlockSpec(memory_space=pltpu.VMEM)
    out, up_grad, tile_grad = pl.pallas_call(
        kernel,
        out_shape=(
            jax.ShapeDtypeStruct((1024, 256), BF),
            jax.ShapeDtypeStruct((256, 2048), BF),
            jax.ShapeDtypeStruct((256, 128), F32),
        ),
        in_specs=[pl.BlockSpec(memory_space=pltpu.SMEM), in_vmem, in_vmem] + [anywhere] * 7,
        out_specs=(in_vmem, anywhere, in_vmem),
        scratch_shapes=[
            vmem((1280, 128), BF), vmem((1280, 128), BF), vmem((256, 1280), F32), vmem((1024, 1024), BF),
            vmem((8, 1024, 256), BF), vmem((1024, 2048), BF), vmem((1024, 256), BF), vmem((256, 256), BF),
            vmem((2, 128, 128), BF), vmem((8, 1024, 256), F32), vmem((2, 7, 512, 256), BF),
            vmem((2, 7, 512, 256), BF), vmem((256, 1024), BF), vmem((1024, 256), BF), vmem((256, 1024), BF), vmem((8, 32, 256), BF), vmem((7, 32, 256), BF),
            vmem((4, 256, 256), BF), vmem((8, 32, 384), F32), vmem((7, 32, 384), F32), vmem((256, 2048), BF),
            vmem((256, 128), F32),
            dma((4, 2)), dma((4, 2)), dma((7,)), dma((2, 7)), dma((2, 7)), dma((3, 4)), dma((3, 4)),
            dma((2, 7)), dma((2, 7)), dma((7,)), dma((7,)), dma((7,)), dma((7,)), dma((3,)), dma((3,)),
            dma((7,)), dma((7,)), dma((7,)), dma((7,)), dma((7,)), dma((7,)), dma((7,)), dma((7,)),
        ],
        compiler_params=pltpu.CompilerParams(
            collective_id=0, has_side_effects=True, vmem_limit_bytes=60 * 1024 * 1024
        ),
    )(
        placement.reshape(2, 2),
        documents,
        queries.reshape(256, 1024),
        keys.reshape(256, 128),
        values.reshape(256, 128),
        weight,
        down,
        up,
        tiles.reshape(2, 128, 128),
        cotangent.reshape(1024, 256),
    )
    steps = 4
    results = ((1024, 256, BF), (256, 2048, F32), (256, 128, F32))
    specs = [pl.BlockSpec((rows // steps, lanes), lambda i: (i, 0)) for rows, lanes, _ in results]
    out, up_grad, tile_grad = pl.pallas_call(
        hand_over,
        grid=(steps,),
        out_shape=tuple(jax.ShapeDtypeStruct((rows, lanes), kind) for rows, lanes, kind in results),
        in_specs=specs,
        out_specs=tuple(specs),
    )(out, up_grad, tile_grad)
    return (
        out.reshape(4, 256, 256),
        up_grad,
        tile_grad.reshape(1, 1, 2, 128, 128),
    )


def solution(mesh):
    placed = (
        P("row", "seq", "col"),
        P("row", "seq", "col"),
        P("row", "seq", "col"),
        P("row", None),
        P("col", "row"),
        P("col", None),
        P(None, "row"),
        P("row", "col", None, None, None),
        P("row", "col", None, None),
        P(None, "seq", ("row", "col")),
    )
    return jax.shard_map(
        local,
        mesh=mesh,
        in_specs=placed,
        out_specs=(
            P(None, "seq", ("row", "col")),
            P(None, "row"),
            P("row", "col", None, None, None),
        ),
        check_vma=False,
    )
```

```python
import functools

import jax
import jax.numpy as jnp
from jax import lax
from jax.experimental import pallas as pl
from jax.experimental.pallas import tpu as pltpu
from jax.sharding import PartitionSpec as P

HEAD_WIDTH = 128
TILE = 128
MESH = pl.DeviceIdType.MESH
BF = jnp.bfloat16
F32 = jnp.float32
LOW_RANK_FACTOR = 2.0
EXP_SCALE = HEAD_WIDTH ** -0.5 * 1.4426950408889634
HIDDEN = -1e30


def dot(a, b, dims=((1,), (0,))):
    return lax.dot_general(a, b, (dims, ((), ())), preferred_element_type=F32)


def kernel(
    place, doc, q, k_hbm, v_hbm, w_hbm, d_hbm, u_hbm, t_hbm, cot_hbm,
    out, up_out, gt_out,
    kwin, vwin, vt, bias, attn, cotall, w, d, u, tiles, cblk, snd, rcv, choice, picked, picked_t, lr_part, lr_recv, lr_full,
    sum_src, sum_recv, up_full, gt_full,
    kv_s, kv_r, loc, cot_s, cot_r, row_s, row_r, rs_s, rs_r, lr_s, lr_r, lb_s, lb_r, lw_s, lw_r,
    ss_s, ss_r, uz_s, uz_r, us_s, us_r, gs_s, gs_r,
):
    r, c, s = lax.axis_index("row"), lax.axis_index("col"), lax.axis_index("seq")

    def remote(src, dst, send, recv, row=None, col=None, seq=None):
        return pltpu.make_async_remote_copy(
            src_ref=src,
            dst_ref=dst,
            send_sem=send,
            recv_sem=recv,
            device_id=(r if row is None else row, c if col is None else col, s if seq is None else seq),
            device_id_type=MESH,
        )

    def mul(x, n):
        return pl.multiple_of(x * n, n)

    barrier = pltpu.get_barrier_semaphore()
    for o in range(1, 8):
        pl.semaphore_signal(barrier, inc=1, device_id=(r, c, (s + o) % 8), device_id_type=MESH)
        pl.semaphore_signal(barrier, inc=1, device_id=(r, (c + o) % 8, s), device_id_type=MESH)
    for o in range(1, 4):
        pl.semaphore_signal(barrier, inc=1, device_id=((r + o) % 4, c, s), device_id_type=MESH)
    pl.semaphore_wait(barrier, 17)

    kv = []
    for j in (1, 2, 3, 4):
        at = pl.ds((4 - j) * 256, 256)
        kv.append(remote(k_hbm, kwin.at[at], kv_s.at[j - 1, 0], kv_r.at[j - 1, 0], seq=(s + j) % 8))
        kv.append(remote(v_hbm, vwin.at[at], kv_s.at[j - 1, 1], kv_r.at[j - 1, 1], seq=(s + j) % 8))
        kv[-2].start()
        kv[-1].start()

    cot_order = [[(1, 0), (1, 1), (2, 0), (2, 1), (3, 0), (3, 1), (4, 0)],
                 [(1, 1), (1, 0), (2, 1), (2, 0), (3, 1), (3, 0), (4, 1)]]
    signs = (1, -1)

    def cot_copy(way, m):
        step, half = cot_order[way][m]
        owner = (c - signs[way] * (step - 1) + 8) % 8
        rows = pl.ds(half * 512, 512)
        src = cot_hbm.at[rows] if step == 1 else cotall.at[owner, rows]
        return remote(src, cotall.at[owner, rows], cot_s.at[way, m], cot_r.at[way, m],
                      col=(c + signs[way] + 8) % 8)

    cot = [[cot_copy(way, m) for m in range(7)] for way in range(2)]
    for m in range(2):
        for way in range(2):
            cot[way][m].start()

    def cot_forward(m):
        for way in range(2):
            cot[way][m].wait_recv()
            cot[way][m + 2].start()

    locals_ = [
        pltpu.make_async_copy(src, dst, loc.at[i])
        for i, (src, dst) in enumerate(
            (
                (k_hbm, kwin.at[pl.ds(1024, 256)]),
                (v_hbm, vwin.at[pl.ds(1024, 256)]),
                (d_hbm, d),
                (cot_hbm, cotall.at[c]),
                (t_hbm, tiles),
                (u_hbm.at[:, pl.ds(mul(c, 256), 256)], u),
                (w_hbm, w),
            )
        )
    ]
    for copy in locals_:
        copy.start()

    own_doc = doc[:, pl.ds(mul(s, 256), 256)].astype(F32)
    for slot in range(5):
        block = s - 4 + slot
        key_doc = doc[:, pl.ds(mul((block + 8) % 8, 256), 256)].astype(F32)
        column = jnp.broadcast_to(key_doc, (128, 256)).T
        column = jnp.concatenate([column, column], axis=1)
        key_at = block * 256 + lax.broadcasted_iota(jnp.int32, (256, 256), 0)
        query_at = s * 256 + lax.broadcasted_iota(jnp.int32, (256, 256), 1)
        seen = (key_at >= 0) & (key_at <= query_at) & (column == own_doc)
        bias[slot * 256 : slot * 256 + 256, :] = jnp.where(seen, 0.0, HIDDEN)

    for t in range(2):
        row = lax.broadcasted_iota(jnp.int32, (128, 1024), 0)
        lane = lax.broadcasted_iota(jnp.int32, (128, 1024), 1)
        wanted = jnp.full((128, 1024), place[t, 0], jnp.int32) * 128 + row
        choice[t * 128 : t * 128 + 128, :] = jnp.where(lane == wanted, 1.0, 0.0).astype(BF)

    locals_[0].wait()
    locals_[1].wait()
    for copy in kv[:4]:
        copy.wait_recv()
    cot_forward(0)
    for copy in kv[4:]:
        copy.wait_recv()

    vt[...] = vwin[...].astype(F32).T.astype(BF)
    own_rows = pl.ds(mul(r, 256), 256)

    def head(h):
        at = slice(h * 128, h * 128 + 128)
        scores = dot(kwin[...], q[:, at], ((1,), (1,))) + bias[...]
        top = jnp.max(scores, axis=0, keepdims=True)
        probs = jnp.exp2((scores - top) * EXP_SCALE)
        total = jnp.sum(probs, axis=0, keepdims=True)
        mixed = dot(vt[...], probs.astype(BF)) / total
        attn[own_rows, at] = mixed.T.astype(BF)

    sibling, opposite = r + 1 - 2 * (r % 2), (r + 2) % 4
    shared, crossed, relayed = [], [], []
    for p in range(4):
        lanes = pl.ds(p * 256, 256)
        mine = attn.at[own_rows, lanes]
        other = attn.at[pl.ds(mul(opposite, 256), 256), lanes]
        shared.append(remote(mine, mine, row_s.at[0, p], row_r.at[0, p], row=sibling))
        crossed.append(remote(mine, mine, row_s.at[1, p], row_r.at[1, p], row=opposite))
        relayed.append(remote(other, other, row_s.at[2, p], row_r.at[2, p], row=sibling))

    def relay(p):
        crossed[p].wait_recv()
        relayed[p].start()

    for p in range(4):
        head(2 * p)
        head(2 * p + 1)
        crossed[p].start()
        shared[p].start()
        if p == 0:
            cot_forward(1)
        if p == 2:
            cot_forward(2)

    locals_[2].wait()
    lr_part[...] = dot(attn[own_rows, :], d[...]).astype(BF).reshape(8, 32, 256)
    lr = [
        remote(lr_part.at[(c + o) % 8], lr_recv.at[o - 1], lr_s.at[o - 1], lr_r.at[o - 1], col=(c + o) % 8)
        for o in range(1, 8)
    ]
    for copy in lr:
        copy.start()
    relay(0)
    relay(1)
    for copy in lr:
        copy.wait_recv()
    piece_at = pl.ds(mul(c, 32), 32)
    lr_full[r, piece_at, :] = (lr_part[c].astype(F32) + jnp.sum(lr_recv[...].astype(F32), axis=0)).astype(BF)
    piece = lr_full.at[r, piece_at]
    lb = [remote(piece, piece, lb_s.at[o - 1], lb_r.at[o - 1], col=(c + o) % 8) for o in range(1, 8)]
    for copy in lb:
        copy.start()
    cot_forward(3)
    relay(2)
    relay(3)
    for copy in lb:
        copy.wait_recv()
    lw = [remote(lr_full.at[r], lr_full.at[r], lw_s.at[o - 1], lw_r.at[o - 1], row=(r + o) % 4) for o in range(1, 4)]
    for copy in lw:
        copy.start()
    cot_forward(4)

    for copy in shared + relayed:
        copy.wait_recv()
    for copy in locals_[3:]:
        copy.wait()

    def pick(h, carry):
        rows = pl.ds(mul(h, 512), 512)
        picked[rows, :] = dot(attn[rows, :], choice[...], ((1,), (1,))).astype(BF)
        picked_t[:, rows] = dot(choice[...], attn[rows, :], ((1,), (1,))).astype(BF)
        return carry

    lax.fori_loop(0, 2, pick, 0)

    def partial(o):
        block = (c + o) % 8
        grid = []
        for t in range(2):
            at = jnp.full((128, 128), place[t, 1], jnp.int32)
            tile = tiles[t].astype(F32)
            grid.append(
                jnp.concatenate([jnp.where(at == 2 * block + i, tile, 0.0) for i in range(2)], axis=1)
            )
        placed = jnp.concatenate(grid, axis=0).astype(BF)
        lanes = pl.ds(mul(block, 256), 256)

        def half(h, carry):
            rows = pl.ds(mul(h, 512), 512)
            cblk[o, rows, :] = dot(attn[rows, :], w[:, lanes]) + dot(picked[rows, :], placed)
            return carry

        lax.fori_loop(0, 2, half, 0)

    def rs_order(way):
        p, n = (0, 1) if way == 0 else (1, 0)
        return [(1, p), (2, n), (2, p), (3, n), (3, p), (4, n), (4, p)]

    rs = [
        [
            remote(snd.at[way, m], rcv.at[way, m], rs_s.at[way, m], rs_r.at[way, m], col=(c + signs[way] + 8) % 8)
            for m in range(7)
        ]
        for way in range(2)
    ]

    def rs_send(m):
        for way in range(2):
            step, half = rs_order(way)[m]
            o = (signs[way] * (5 - step)) % 8
            if m >= 2:
                rs[way][m - 2].wait_recv()

            def chunk(i, carry):
                rows = pl.ds(mul(i, 128), 128)
                value = cblk[o, pl.ds(half * 512 + mul(i, 128), 128), :]
                if m >= 2:
                    value = value + rcv[way, m - 2, rows, :].astype(F32)
                snd[way, m, rows, :] = value.astype(BF)
                return carry

            lax.fori_loop(0, 4, chunk, 0)
            rs[way][m].start()

    partial(4)
    rs_send(0)
    partial(3)
    partial(5)
    rs_send(1)

    for copy in lw:
        copy.wait_recv()
    up_piece = LOW_RANK_FACTOR * dot(lr_full[...].reshape(1024, 256), cotall[c], ((0,), (0,)))
    sum_src[:, :, :256] = up_piece.reshape(8, 32, 256)
    partial(2)
    partial(6)
    for m in (5, 6):
        for way in range(2):
            cot[way][m].wait_recv()
    rs_send(2)

    def tile_grads(owner, carry):
        grads = dot(picked_t[...], cotall[owner])
        kept = []
        for t in range(2):
            value = carry[t]
            for i in range(2):
                at = jnp.full((128, 128), place[t, 1], jnp.int32)
                part = grads[t * 128 : t * 128 + 128, i * 128 : i * 128 + 128]
                value = jnp.where(at == 2 * owner + i, part, value)
            kept.append(value)
        return tuple(kept)

    grads = lax.fori_loop(0, 8, tile_grads, (jnp.zeros((128, 128), F32),) * 2)
    for t in range(2):
        sum_src[t * 4 : t * 4 + 4, :, 256:] = grads[t].reshape(4, 32, 128)
    ss = [
        remote(sum_src.at[(s + o) % 8], sum_recv.at[o - 1], ss_s.at[o - 1], ss_r.at[o - 1], seq=(s + o) % 8)
        for o in range(1, 8)
    ]
    for copy in ss:
        copy.start()
    rs_send(3)
    partial(1)
    partial(7)
    for copy in ss:
        copy.wait_recv()
    total = sum_src[s] + jnp.sum(sum_recv[...], axis=0)
    seq_rows = pl.ds(mul(s, 32), 32)
    col_lanes = pl.ds(mul(c, 256), 256)
    up_full[seq_rows, col_lanes] = total[:, :256].astype(BF)
    gt_full[seq_rows, :] = total[:, 256:]
    up_at, gt_at = up_full.at[seq_rows, col_lanes], gt_full.at[seq_rows]
    uz = [remote(up_at, up_at, uz_s.at[o - 1], uz_r.at[o - 1], col=(c + o) % 8) for o in range(1, 8)]
    gs = [remote(gt_at, gt_at, gs_s.at[o - 1], gs_r.at[o - 1], seq=(s + o) % 8) for o in range(1, 8)]
    for copy in uz + gs:
        copy.start()
    rs_send(4)
    partial(0)

    def low_rank_half(h, carry):
        rows = pl.ds(mul(h, 512), 512)
        inner = lr_full[pl.ds(2 * h, 2)].reshape(512, 256)
        cblk[0, rows, :] = cblk[0, rows, :] + LOW_RANK_FACTOR * dot(inner, u[...])
        return carry

    lax.fori_loop(0, 2, low_rank_half, 0)
    for copy in uz:
        copy.wait_recv()
    seq_at = up_full.at[seq_rows]
    us = [remote(seq_at, seq_at, us_s.at[o - 1], us_r.at[o - 1], seq=(s + o) % 8) for o in range(1, 8)]
    for copy in us:
        copy.start()
    rs_send(5)
    rs_send(6)
    for copy in us + gs:
        copy.wait_recv()
    gt_out[...] = gt_full[...]
    up_copy = pltpu.make_async_copy(up_full, up_out, loc.at[0])
    up_copy.start()
    for m in (5, 6):
        for way in range(2):
            rs[way][m].wait_recv()

    def finish(i, carry):
        for half in range(2):
            rows = pl.ds(mul(i, 128), 128)
            at = pl.ds(half * 512 + mul(i, 128), 128)
            there = [rcv[way, 6 if half == way else 5, rows, :].astype(F32) for way in range(2)]
            out[at, :] = (cblk[0, at, :] + (there[0] + there[1])).astype(BF)
        return carry

    lax.fori_loop(0, 4, finish, 0)
    up_copy.wait()
    for copy in kv + cot[0] + cot[1] + shared + crossed + relayed + lr + lb + lw + rs[0] + rs[1] + ss + uz + gs + us:
        copy.wait_send()


def hand_over(out, up_grad, tile_grad, out_to, up_to, tile_to):
    out_to[...] = out[...]
    up_to[...] = up_grad[...].astype(F32)
    tile_to[...] = tile_grad[...]


def local(queries, keys, values, documents, weight, down, up, tiles, placement, cotangent):
    dma = pltpu.SemaphoreType.DMA
    vmem = pltpu.VMEM
    anywhere = pl.BlockSpec(memory_space=pl.ANY)
    in_vmem = pl.BlockSpec(memory_space=pltpu.VMEM)
    out, up_grad, tile_grad = pl.pallas_call(
        kernel,
        out_shape=(
            jax.ShapeDtypeStruct((1024, 256), BF),
            jax.ShapeDtypeStruct((256, 2048), BF),
            jax.ShapeDtypeStruct((256, 128), F32),
        ),
        in_specs=[pl.BlockSpec(memory_space=pltpu.SMEM), in_vmem, in_vmem] + [anywhere] * 7,
        out_specs=(in_vmem, anywhere, in_vmem),
        scratch_shapes=[
            vmem((1280, 128), BF), vmem((1280, 128), BF), vmem((128, 1280), BF), vmem((1280, 256), F32), vmem((1024, 1024), BF),
            vmem((8, 1024, 256), BF), vmem((1024, 2048), BF), vmem((1024, 256), BF), vmem((256, 256), BF),
            vmem((2, 128, 128), BF), vmem((8, 1024, 256), F32), vmem((2, 7, 512, 256), BF),
            vmem((2, 7, 512, 256), BF), vmem((256, 1024), BF), vmem((1024, 256), BF), vmem((256, 1024), BF), vmem((8, 32, 256), BF), vmem((7, 32, 256), BF),
            vmem((4, 256, 256), BF), vmem((8, 32, 384), F32), vmem((7, 32, 384), F32), vmem((256, 2048), BF),
            vmem((256, 128), F32),
            dma((4, 2)), dma((4, 2)), dma((7,)), dma((2, 7)), dma((2, 7)), dma((3, 4)), dma((3, 4)),
            dma((2, 7)), dma((2, 7)), dma((7,)), dma((7,)), dma((7,)), dma((7,)), dma((3,)), dma((3,)),
            dma((7,)), dma((7,)), dma((7,)), dma((7,)), dma((7,)), dma((7,)), dma((7,)), dma((7,)),
        ],
        compiler_params=pltpu.CompilerParams(
            collective_id=0, has_side_effects=True, vmem_limit_bytes=60 * 1024 * 1024
        ),
    )(
        placement.reshape(2, 2),
        documents,
        queries.reshape(256, 1024),
        keys.reshape(256, 128),
        values.reshape(256, 128),
        weight,
        down,
        up,
        tiles.reshape(2, 128, 128),
        cotangent.reshape(1024, 256),
    )
    steps = 2
    results = ((1024, 256, BF), (256, 2048, F32), (256, 128, F32))
    specs = [pl.BlockSpec((rows // steps, lanes), lambda i: (i, 0)) for rows, lanes, _ in results]
    out, up_grad, tile_grad = pl.pallas_call(
        hand_over,
        grid=(steps,),
        out_shape=tuple(jax.ShapeDtypeStruct((rows, lanes), kind) for rows, lanes, kind in results),
        in_specs=specs,
        out_specs=tuple(specs),
    )(out, up_grad, tile_grad)
    return (
        out.reshape(4, 256, 256),
        up_grad,
        tile_grad.reshape(1, 1, 2, 128, 128),
    )


def solution(mesh):
    placed = (
        P("row", "seq", "col"),
        P("row", "seq", "col"),
        P("row", "seq", "col"),
        P("row", None),
        P("col", "row"),
        P("col", None),
        P(None, "row"),
        P("row", "col", None, None, None),
        P("row", "col", None, None),
        P(None, "seq", ("row", "col")),
    )
    return jax.shard_map(
        local,
        mesh=mesh,
        in_specs=placed,
        out_specs=(
            P(None, "seq", ("row", "col")),
            P(None, "row"),
            P("row", "col", None, None, None),
        ),
        check_vma=False,
    )
```
